32 devices in a mesh: expert: 8 (over z, y), tensor: 4 (over x, core).
Axes of the slice: x: 2, y: 2, z: 4, core: 2. Of those that a mesh axis runs over, the one named last changes fastest.
Arguments:
- attn_partial: bfloat16 [4, 2048, 7168], P('tensor', 'expert'), may hold values from -4 to 4
- residual: bfloat16 [2048, 7168], P(('expert', 'tensor')), may hold values from -6 to 6
- norm_gain: float32 [7168], replicated, may hold values from 0.25 to 1.75
- channel_order: int32 [7168], replicated, may hold values from 0 to 7167, each once
- rotation: bfloat16 [56, 128, 128], replicated, may hold values from -0.5 to 0.5
- routes: int32 [2048, 8], P(('expert', 'tensor')), may hold values from 0 to 31, all different within a row; in each aligned block of 64 rows (0 to 63, 64 to 127, ...) at most 24 rows name the same one
- slab_block: int32 [32], P(('expert', 'tensor')), may hold values from 0 to 52
Outputs:
- hessian: bfloat16 [32, 7168, 512], P(('expert', 'tensor'))
The draws below stay inside these ranges and needn't reach their ends.
Inputs may be any that keep to these rules, and one draw needn't show every extreme that they name: `routes`: tokens are numbered in the order of their devices along expert+tensor, 256 // 4 a device. Each token names 8 different experts; every expert is named by some token; the tokens of one device name one expert at most 24 times, and exactly 24 times somewhere.
All inputs are finite; a program needn't handle non-finite values.
Results may differ from the reference program's by a relative error of at most 0.018.
Values may be sent and summed in bfloat16 or wider, within the bound.
A program may use at most 128 MiB of HBM per device.

```python
import math
import jax
import jax.numpy as jnp
import numpy as np
from jax import lax

D = 7168
TOP = 8
BLK = 128
SLAB = 512
TOK_DEV = 256
EXPERTS = 32
TOKENS = 2048
CAP = 24
N_EXPERT = 8
N_TENSOR = 4


def with_ends(array, own_key, least, largest):
    longest = array.shape.index(max(array.shape))
    spots = []
    for shift in (0, 1):
        where = [jax.random.randint(jax.random.fold_in(own_key, axis), (), 0, length) for axis, length in enumerate(array.shape)]
        where[longest] = (where[longest] + shift) % array.shape[longest]
        spots.append(tuple(where))
    return array.at[spots[0]].set(least).at[spots[1]].set(largest)


def spiked(drawn, own_key, source, target, blocks, factor):
    def block_of(axis_at):
        return (jnp.arange(drawn.shape[axis_at]) // (drawn.shape[axis_at] // blocks)).reshape((-1,) + (1,) * (drawn.ndim - 1 - axis_at))

    first = jax.random.permutation(own_key, blocks)[block_of(target)]
    other_side = (block_of(target) + blocks // 2) % blocks
    return jnp.where((block_of(source) == first) | (block_of(source) == other_side), factor * drawn, drawn)


def block_scale(rng, extent, split, least, largest):
    gain = 1.0
    for axis_at, blocks in split:
        draws = jax.random.uniform(jax.random.fold_in(jax.random.fold_in(rng, 6), axis_at), (blocks,), jnp.float32, least / len(split), largest / len(split))
        gain = gain * jnp.repeat(jnp.exp(draws), extent[axis_at] // blocks).reshape((-1,) + (1,) * (len(extent) - 1 - axis_at))
    return gain


def routed_block(own_key, own, number, rows, number_of, top, reach, slope):
    ranking = jax.random.permutation(own_key, number_of)
    packed, ordinary = load_shares(number_of, rows * top, reach, slope, True), load_shares(number_of, rows * top, reach, slope, False)
    places = jnp.arange(number_of)

    def named(tallies, turn):
        used = int((tallies > 0).sum())
        fixed = max(1, used // 4)
        moved = fixed + (places - fixed + turn * (used - fixed)) % max(1, number_of - fixed)
        return jnp.zeros((number_of,), jnp.int32).at[ranking[jnp.where(places < fixed, places, moved)]].set(jnp.asarray(tallies, jnp.int32))

    tallies = jnp.where(number % 4 == 0, named(packed, number // 4), named(ordinary, number - number // 4 - 1))
    mixed = jax.random.permutation(jax.random.fold_in(own, 3), number_of)
    giver, sink = mixed[0:number_of // 2 * 2:2], mixed[1:number_of // 2 * 2:2]
    slack = jnp.minimum(tallies[giver] - 1, reach - tallies[sink]) // 2
    slack = jnp.where((giver == ranking[0]) | (sink == ranking[0]) | (tallies[sink] == 0), 0, jnp.maximum(slack, 0))
    moved = jax.random.randint(jax.random.fold_in(own, 4), (number_of // 2,), 0, 1 << 20) % (slack + 1)
    tallies = tallies.at[giver].add(-moved).at[sink].add(moved)
    items = jnp.searchsorted(jnp.cumsum(tallies), jnp.arange(rows * top), side="right").astype(jnp.int32)
    table = items.reshape(top, rows).T
    table = table[jax.random.permutation(jax.random.fold_in(own, 1), rows)]
    turn = jax.random.randint(jax.random.fold_in(own, 2), (rows, 1), 0, top)
    return jnp.take_along_axis(table, (jnp.arange(top)[None, :] + turn) % top, axis=1)


def load_shares(amount, total, most, slope, full):
    loads = [(1 << 20) // math.isqrt(grade ** slope) + 1 for grade in range(1, amount + 1)]
    largest = most if full else min(most, max(-(-total // amount), total * loads[0] // sum(loads)))
    least = 1 if total - largest >= amount - 1 else 0
    holding, rest = [largest] + [least] * (amount - 1), total - largest - least * (amount - 1)
    while rest > 0:
        free = [i for i in range(1, amount) if holding[i] < largest] or [i for i in range(1, amount) if holding[i] < most]
        pool, budget = sum([loads[i] for i in free]), rest
        for i in free:
            extra = min(most - holding[i], max(1, budget * loads[i] // pool), rest)
            holding[i] = holding[i] + extra
            rest = rest - extra
    return np.array(holding)


def centred(stream_key, shape, spread, bound, shards=(), kind=jnp.bfloat16):
    values = spread * jax.random.normal(stream_key, shape, jnp.float32)
    if shards:
        values = values * block_scale(stream_key, shape, shards, -0.22, 0.18)
    return jnp.clip(values, -bound, bound).astype(kind)


def bell_draw_with(stream_key, shape, width, reach, cuts, heavy, kind=jnp.bfloat16):
    drawn = width * jax.random.normal(stream_key, shape, jnp.float32)
    if cuts:
        drawn = drawn * block_scale(stream_key, shape, cuts, -0.22, 0.18)
    return jnp.clip(spiked(drawn, jax.random.fold_in(stream_key, 3), *heavy), -reach, reach).astype(kind)


def setup_inputs(seed: int = 0) -> dict:
    arg_keys = jax.random.split(jax.random.key(seed), 8)
    attn_partial = bell_draw_with(arg_keys[0], (N_TENSOR, TOKENS, D), 0.5, 4.0, ((0, 4), (1, 8)), (0, 1, 4, 2.0))
    residual = centred(arg_keys[1], (TOKENS, D), 1.0, 6.0, ((0, 32),))
    norm_gain = jnp.clip(1.0 + 0.15 * jax.random.normal(arg_keys[2], (D,), jnp.float32), 0.25, 1.75)
    channel_order = jax.random.permutation(arg_keys[3], D).astype(jnp.int32)
    rotation = centred(arg_keys[4], (D // BLK, BLK, BLK), BLK ** -0.5, 0.5)
    routes_keys = jax.random.split(jax.random.fold_in(arg_keys[5], 1), TOKENS // (TOK_DEV // N_TENSOR))
    routes_turns = jax.random.permutation(jax.random.fold_in(arg_keys[5], 3), TOKENS // (TOK_DEV // N_TENSOR))
    routes = jax.vmap(lambda own, number: routed_block(jax.random.fold_in(arg_keys[5], 2), own, number, TOK_DEV // N_TENSOR, EXPERTS, TOP, CAP, 2))(routes_keys, routes_turns).reshape((TOKENS, TOP))
    slab_block = with_ends(jax.random.randint(arg_keys[6], (EXPERTS,), 0, D // BLK - SLAB // BLK + 1), jax.random.fold_in(arg_keys[6], 1), 0, (D // BLK - SLAB // BLK + 1) - 1).astype(jnp.int32)
    return dict(attn_partial=attn_partial, residual=residual, norm_gain=norm_gain, channel_order=channel_order, rotation=rotation, routes=routes, slab_block=slab_block)


def rotate_rows(rows, channel_order, rotation):
    moved = jnp.take(rows, channel_order, axis=1)
    blocks = moved.reshape(rows.shape[0], rotation.shape[0], rotation.shape[1]).astype(jnp.float32)
    out = jnp.einsum('rbi,bij->rbj', blocks, rotation.astype(jnp.float32))
    return out.reshape(rows.shape[0], -1).astype(jnp.bfloat16)

def reference(attn_partial, residual, norm_gain, channel_order, rotation, routes, slab_block):
    attn = lax.optimization_barrier(jnp.sum(attn_partial.astype(jnp.float32), axis=0))
    hidden = residual.astype(jnp.float32) + attn
    scale = lax.rsqrt(lax.optimization_barrier(jnp.mean(hidden * hidden, axis=1, keepdims=True)) + 1e-06)
    normed = (hidden * scale * norm_gain[None, :]).astype(jnp.bfloat16)
    rotated = rotate_rows(normed, channel_order, rotation)
    limit = CAP * N_EXPERT * N_TENSOR
    expert_ids = jnp.arange(EXPERTS, dtype=jnp.int32)

    def one_expert(args):
        expert_id, block_id = args
        chosen = jnp.any(routes == expert_id, axis=1)
        keys = jnp.where(chosen, 0, 1).astype(jnp.int32)
        picked = jnp.argsort(keys, stable=True)[:limit].astype(jnp.int32)
        rows = rotated[picked] * chosen[picked][:, None].astype(jnp.bfloat16)
        count = jnp.sum(chosen.astype(jnp.float32))
        start = (block_id * BLK).astype(jnp.int32)
        slab = lax.dynamic_slice_in_dim(rows, start, SLAB, 1)
        product = lax.dot_general(rows, slab, (((0,), (0,)), ((), ())), preferred_element_type=jnp.float32)
        return (product * (2.0 / count)).astype(jnp.bfloat16)
    return lax.map(one_expert, (expert_ids, slab_block))
```

```python
import functools

import jax
import jax.numpy as jnp
from jax import lax
from jax.experimental import pallas as pl
from jax.experimental.pallas import tpu as pltpu
from jax.sharding import PartitionSpec as P

SLAB = 512


def rotate_rows(rows, channel_order, rotation):
    moved = jnp.take(rows, channel_order, axis=1)
    blocks = moved.reshape(rows.shape[0], rotation.shape[0], rotation.shape[1])
    out = jnp.einsum("rbi,bij->rbj", blocks, rotation, preferred_element_type=jnp.float32)
    return out.reshape(rows.shape[0], -1).astype(jnp.bfloat16)


def dispatch_rows(payload, routes):
    count_expert = lax.axis_size("expert")
    count_tensor = lax.axis_size("tensor")
    experts = count_expert * count_tensor
    local_rows = payload.shape[0]
    mean_load = local_rows * routes.shape[1] // experts
    slots = max(2, mean_load + (mean_load + 1) // 2)
    expert_ids = jnp.arange(experts, dtype=jnp.int32)
    chosen = jnp.any(routes[:, :, None] == expert_ids[None, None, :], axis=1)
    ranks = jnp.cumsum(chosen.astype(jnp.int32), axis=0) - 1
    slot_ids = jnp.arange(slots, dtype=jnp.int32)
    select = (chosen[:, :, None] & (ranks[:, :, None] == slot_ids[None, None, :])).astype(
        jnp.bfloat16
    )
    occupancy = jnp.sum(select.astype(jnp.float32), axis=0).astype(jnp.bfloat16)
    outgoing = jnp.einsum(
        "rec,rd->ecd", select, payload, preferred_element_type=jnp.float32
    ).astype(jnp.bfloat16)
    outgoing = outgoing.reshape(count_expert, count_tensor, slots, payload.shape[1])
    occupancy = occupancy.reshape(count_expert, count_tensor, slots)
    arrived, filled = (
        lax.all_to_all(
            lax.all_to_all(outgoing, "expert", split_axis=0, concat_axis=0, tiled=True),
            "tensor",
            split_axis=1,
            concat_axis=1,
            tiled=True,
        ),
        lax.all_to_all(
            lax.all_to_all(occupancy, "expert", split_axis=0, concat_axis=0, tiled=True),
            "tensor",
            split_axis=1,
            concat_axis=1,
            tiled=True,
        ),
    )
    rows = arrived.reshape(-1, payload.shape[1])
    count = jnp.sum(filled.astype(jnp.float32))
    return rows, count


def line_order(length):
    orders = []
    for at in range(length):
        near = -1 if 2 * at < length else 1
        hops = [d for far in range(1, length) for d in (near * far, -near * far)]
        orders.append([at + d for d in hops if 0 <= at + d < length])
    return orders


def plan(planes):
    ops = []
    own = ("own", 0)
    turns = [("turn", k) for k in range(planes - 1)]

    def wait(z, dx, dy, kind, part=None, other=0):
        ops.append(("wait", z, dx, dy, other, kind, part))

    def send(z, dx, dy, kind, part, *ways):
        for way in ways:
            ops.append(("send", z, dx, dy, kind, part, way))

    def ways_of(kind):
        return ("z+", "z-", "c") if kind == 2 else ("c",)

    def relay(z, kind):
        wait(z, 1, 0, kind)
        send(z, 1, 0, kind, 0, "y")
        send(z, 1, 0, kind, None, *ways_of(kind))
        wait(z, 0, 1, kind)
        send(z, 0, 1, kind, 1, "x")
        send(z, 0, 1, kind, None, *ways_of(kind))

    def diagonal(z, kind):
        wait(z, 1, 1, kind, 0)
        wait(z, 1, 1, kind, 1)
        send(z, 1, 1, kind, None, *ways_of(kind))

    def take(far, kind):
        for dx, dy in ((0, 0), (1, 0), (0, 1), (1, 1)) if kind == 2 else ((0, 0),):
            for step in (-far, far):
                wait(("dist", step), dx, dy, kind)
                send(("dist", step), dx, dy, kind, None, "z+" if step < 0 else "z-", "c")

    def spread(z):
        for kind in (0, 1):
            send(z, 0, 0, kind, None, "y", "x")

    def gram(z, dy):
        for kind in (0, 1, 2):
            for dx in (0, 1):
                wait(z, dx, dy, kind, None, 1)
        ops.append(("gram", z, dy))

    ops.append(("chunk", 0))
    send(own, 0, 0, 0, None, "z+", "z-", "y", "x", "c")
    ops.append(("chunk", 1))
    send(own, 0, 0, 1, None, "z+", "z-")
    send(own, 0, 0, 2, None, "y", "x", "z+", "z-")
    send(own, 0, 0, 1, None, "y", "x", "c")
    send(own, 0, 0, 2, None, "c")
    relay(own, 0)
    take(1, 0)
    relay(own, 2)
    relay(own, 1)
    take(1, 1)
    spread(turns[0])
    for kind in (2, 0, 1):
        diagonal(own, kind)
    take(1, 2)
    for k in range(planes - 1):
        before = own if k == 0 else turns[k - 1]
        relay(turns[k], 0)
        gram(before, 0)
        if k + 2 < planes:
            take(k + 2, 0)
        relay(turns[k], 1)
        if k + 2 < planes:
            take(k + 2, 1)
            spread(turns[k + 1])
        gram(before, 1)
        diagonal(turns[k], 0)
        diagonal(turns[k], 1)
        if k + 2 < planes:
            take(k + 2, 2)
    gram(turns[-1], 0)
    gram(turns[-1], 1)
    return ops


def divisor(number, most):
    return max(d for d in range(1, most + 1) if number % d == 0)


def hessian_kernel(
    planes, local, width, columns, extra,
    order_ref, block_ref, partial_ref, residual_ref, gain_ref, routes_ref, rotation_ref, out_ref,
    rows, total, staged, picked, slab, split, rotation, mid, far, residual, moved,
    load_sem, core_send, core_recv, pair_send, pair_recv, send_sem, recv_sem, half_sem, out_sem,
):
    expert, tensor = lax.axis_index("expert"), lax.axis_index("tensor")
    plane, side = lax.div(expert, 2), lax.rem(expert, 2)
    pair, core = lax.div(tensor, 2), lax.rem(tensor, 2)
    me = expert * 4 + tensor
    half = local // 2
    orders = line_order(planes)

    def table(values):
        total_of = 0
        for at, value in enumerate(values):
            total_of = total_of + value * lax.div(
                planes - lax.rem(plane + planes - at, planes), planes
            )
        return total_of

    def device(z, y, x, c):
        return (z * 2 + y, x * 2 + c)

    def remote(source, target, send, recv, to):
        return pltpu.make_async_remote_copy(
            src_ref=source, dst_ref=target, send_sem=send, recv_sem=recv,
            device_id=to, device_id_type=pl.DeviceIdType.MESH,
        )

    other_pair = device(plane, side, 1 - pair, core)
    other_side = device(plane, 1 - side, pair, core)
    other_core = device(plane, side, pair, 1 - core)

    def beside(step):
        there = table([1 if 0 <= at + step < planes else 0 for at in range(planes)])
        return there, table([min(max(at + step, 0), planes - 1) for at in range(planes)])

    parts = 4
    size = local // parts
    mine, got = 0, 2 * local

    def source(p, c, at, count):
        start = pl.multiple_of((p * 2 + c) * local + at, size)
        return partial_ref.at[0, pl.ds(start, count), :]

    loads = [
        pltpu.make_async_copy(
            source(p, core, 0, local),
            picked.at[mine + turn * local:mine + (turn + 1) * local, :],
            load_sem.at[turn],
        )
        for turn, p in enumerate((1 - pair, pair))
    ]
    loads.append(pltpu.make_async_copy(residual_ref, residual, load_sem.at[2]))
    loads.append(pltpu.make_async_copy(rotation_ref, rotation, load_sem.at[3]))
    for copy in loads:
        copy.start()

    barrier = pltpu.get_barrier_semaphore()
    barrier_wait = 3
    for peer in (other_core, other_pair, other_side):
        pl.semaphore_signal(
            barrier, inc=1, device_id=peer, device_id_type=pl.DeviceIdType.MESH
        )
    for step in (-1, 1):
        there, z = beside(step)
        barrier_wait = barrier_wait + there

        @pl.when(there == 1)
        def _():
            pl.semaphore_signal(
                barrier, inc=1, device_id=device(z, side, pair, core),
                device_id_type=pl.DeviceIdType.MESH,
            )

    pl.semaphore_wait(barrier, barrier_wait)

    inside = []
    for turn, p in enumerate((1 - pair, pair)):
        for part in range(parts):
            number = turn * parts + part
            first = got + turn * local + part * size
            inside.append(
                remote(
                    source(p, 1 - core, part * size, size),
                    picked.at[first:first + size, :],
                    core_send.at[number], core_recv.at[number], other_core,
                )
            )
            inside[-1].start()

    named = routes_ref[...]
    lane = lax.broadcasted_iota(jnp.int32, (local, extra), 1)
    chosen = named[:, 0:1] == lane
    for k in range(1, named.shape[1]):
        chosen = chosen | (named[:, k:k + 1] == lane)
    own_rows = pl.ds(pl.multiple_of(me * local, local), local)
    rows[own_rows, width:] = jnp.where(chosen, 1.0, 0.0).astype(jnp.bfloat16)

    across = []
    loads[0].wait()
    for part in range(parts):
        at = slice(part * size, (part + 1) * size)
        inside[part].wait_recv()
        mid[at, :] = (
            picked[mine + part * size:mine + (part + 1) * size, :].astype(jnp.float32)
            + picked[got + part * size:got + (part + 1) * size, :].astype(jnp.float32)
        ).astype(jnp.bfloat16)
        across.append(
            remote(
                mid.at[at, :], far.at[at, :], pair_send.at[part], pair_recv.at[part], other_pair
            )
        )
        if part > 0:
            across[part - 1].start()
    for copy in loads[1:]:
        copy.wait()
    for part in range(parts):
        inside[parts + part].wait_recv()
    across[parts - 1].start()

    blocks = width // columns
    group = divisor(blocks, 14)

    def chunk(q):
        for part in range(q * parts // 2, (q + 1) * parts // 2):
            at = slice(part * size, (part + 1) * size)
            across[part].wait_recv()
            first = local + part * size
            attn = (
                picked[mine + first:mine + first + size, :].astype(jnp.float32)
                + picked[got + first:got + first + size, :].astype(jnp.float32)
                + far[at, :].astype(jnp.float32)
            )
            hidden = residual[at, :].astype(jnp.float32) + attn
            scale = lax.rsqrt(jnp.mean(hidden * hidden, axis=1, keepdims=True) + 1e-06)
            far[at, :] = (hidden * scale * gain_ref[...]).astype(jnp.bfloat16)

        @pl.loop(0, blocks // group)
        def _(b):
            for j in range(group):
                at = pl.ds(pl.multiple_of((b * group + j) * columns, columns), columns)
                total[0, at, 0:half] = far[q * half:(q + 1) * half, at].astype(jnp.float32).T

        place = pl.ds(pl.multiple_of(me * local + q * half, half), half)

        @pl.loop(0, blocks // group)
        def _(b):
            @pl.loop(0, group)
            def _(s):
                base = pl.multiple_of(s * columns, columns)
                origin = (b * group + s) * columns
                for j in range(columns):
                    moved[base + j, :] = total[0, order_ref[origin + j], :]

            for j in range(group):
                at = pl.ds(pl.multiple_of((b * group + j) * columns, columns), columns)
                rows[place, at] = lax.dot_general(
                    moved[j * columns:(j + 1) * columns, 0:half].T.astype(jnp.bfloat16),
                    rotation[b * group + j], (((1,), (0,)), ((), ())),
                    preferred_element_type=jnp.float32,
                ).astype(jnp.bfloat16)

    every = (width + extra) // columns
    late = every * 8 // 19
    spans = (
        (0, 0, every), (1, 0, every - late), (1, every - late, every),
    )

    def plane_of(z):
        if z[0] == "own":
            return None, plane
        if z[0] == "turn":
            return None, table([orders[at][z[1]] for at in range(planes)])
        return beside(z[1])

    def number_of(z, dx, dy, c):
        y = 1 - side if dy else side
        x = 1 - pair if dx else pair
        return (z * 2 + y) * 4 + x * 2 + c

    def piece(number, kind, part):
        h, first, last = spans[kind]
        middle = (first + last) // 2
        if part == 0:
            last = middle
        elif part == 1:
            first = middle
        return rows.at[
            pl.ds(pl.multiple_of(number * local + h * half, half), half),
            first * columns:last * columns,
        ]

    def arrival(z, number, kind, part):
        return recv_sem.at[number, kind] if part is None else half_sem.at[z, kind, part]

    def under(flag, act):
        if flag is None:
            act()
        else:
            pl.when(flag == 1)(act)

    sends = []

    def send(zref, dx, dy, kind, part, way):
        flag, z = plane_of(zref)
        number = number_of(z, dx, dy, core)
        if way in ("z+", "z-"):
            onward, target = beside(1 if way == "z+" else -1)
            flag = onward if flag is None else flag * onward
            to = device(target, side, pair, core)
        else:
            to = {"x": other_pair, "y": other_side, "c": other_core}[way]
        ref = piece(number, kind, part)
        copy = remote(ref, ref, send_sem.at[len(sends)], arrival(z, number, kind, part), to)
        sends.append((flag, copy))
        under(flag, copy.start)

    def arrive(zref, dx, dy, other, kind, part):
        flag, z = plane_of(zref)
        number = number_of(z, dx, dy, 1 - core if other else core)
        ref = piece(number, kind, part)
        copy = remote(ref, ref, send_sem.at[0], arrival(z, number, kind, part), other_core)
        under(flag, copy.wait_recv)

    tile = columns * divisor(blocks, 14)
    last_tile = columns * divisor(blocks, 8)
    begin = block_ref[0]

    def gram(zref, dy, first, last, counted):
        z = plane_of(zref)[1]
        y = 1 - side if dy else side
        base = pl.ds(pl.multiple_of((z * 2 + y) * 4 * local, 4 * local), 4 * local)
        for b in range(blocks):
            split[b, :, :] = rows[base, b * columns:(b + 1) * columns]
        named = rows[base, width:].astype(jnp.float32)
        lane = lax.broadcasted_iota(jnp.int32, named.shape, 1)
        chosen = jnp.sum(jnp.where(lane == me, named, 0.0), axis=1, keepdims=True)
        for b in range(SLAB // columns):
            slab[:, b * columns:(b + 1) * columns] = (
                split[begin + b, :, :].astype(jnp.float32) * chosen
            ).astype(jnp.bfloat16)
        counted = counted + jnp.sum(chosen, axis=0, keepdims=True)
        factor = 2.0 / counted
        wide = last_tile if last else tile

        @pl.loop(0, width // wide)
        def _(step):
            at = pl.ds(pl.multiple_of(step * wide, wide), wide)
            product = lax.dot_general(
                rows[base, at], slab[...], (((0,), (0,)), ((), ())),
                preferred_element_type=jnp.float32,
            )
            for b in range(SLAB // columns):
                lanes = slice(b * columns, (b + 1) * columns)
                if first:
                    total[b, at, :] = product[:, lanes]
                elif not last:
                    total[b, at, :] += product[:, lanes]
                else:
                    staged[at, lanes] = (
                        (total[b, at, :] + product[:, lanes]) * factor
                    ).astype(jnp.bfloat16)
            if last:
                pltpu.make_async_copy(staged.at[at, :], out_ref.at[at, :], out_sem.at[step]).start()

        return counted

    counted = jnp.zeros((1, 1), jnp.float32)
    grams = 0
    for op in plan(planes):
        if op[0] == "chunk":
            chunk(op[1])
        elif op[0] == "send":
            send(*op[1:])
        elif op[0] == "wait":
            arrive(*op[1:])
        else:
            grams += 1
            counted = gram(op[1], op[2], grams == 1, grams == 2 * planes, counted)

    for copy in inside + across:
        copy.wait_send()
    for flag, copy in sends:
        under(flag, copy.wait_send)

    @pl.loop(0, width // last_tile)
    def _(step):
        at = pl.ds(pl.multiple_of(step * last_tile, last_tile), last_tile)
        pltpu.make_async_copy(staged.at[at, :], out_ref.at[at, :], out_sem.at[step]).wait()


def gathered_hessian(
    attn_partial, residual, norm_gain, channel_order, rotation, routes, slab_block
):
    count_expert, count_tensor = lax.axis_size("expert"), lax.axis_size("tensor")
    experts, planes = count_expert * count_tensor, count_expert // 2
    local, width = residual.shape
    blocks, columns = rotation.shape[0], rotation.shape[1]
    extra = -(-experts // columns) * columns
    half = local // 2
    sends = sum(op[0] == "send" for op in plan(planes))
    vmem = pl.BlockSpec(memory_space=pltpu.VMEM)
    smem = pl.BlockSpec(memory_space=pltpu.SMEM)
    whole = pl.BlockSpec(memory_space=pl.ANY)
    return pl.pallas_call(
        functools.partial(hessian_kernel, planes, local, width, columns, extra),
        out_shape=jax.ShapeDtypeStruct((width, SLAB), jnp.bfloat16),
        in_specs=[smem, smem, whole, whole, vmem, vmem, whole],
        out_specs=whole,
        scratch_shapes=[
            pltpu.VMEM((experts * local, width + extra), jnp.bfloat16),
            pltpu.VMEM((SLAB // columns, width, columns), jnp.float32),
            pltpu.VMEM((width, SLAB), jnp.bfloat16),
            pltpu.VMEM((4 * local, width), jnp.bfloat16),
            pltpu.VMEM((4 * local, SLAB), jnp.bfloat16),
            pltpu.VMEM((blocks, 4 * local, columns), jnp.bfloat16),
            pltpu.VMEM(rotation.shape, jnp.bfloat16),
            pltpu.VMEM((local, width), jnp.bfloat16),
            pltpu.VMEM((local, width), jnp.bfloat16),
            pltpu.VMEM((local, width), jnp.bfloat16),
            pltpu.VMEM((columns * divisor(blocks, 14), columns), jnp.float32),
            pltpu.SemaphoreType.DMA((4,)),
            pltpu.SemaphoreType.DMA((8,)),
            pltpu.SemaphoreType.DMA((8,)),
            pltpu.SemaphoreType.DMA((4,)),
            pltpu.SemaphoreType.DMA((4,)),
            pltpu.SemaphoreType.DMA((sends,)),
            pltpu.SemaphoreType.DMA((experts, 3)),
            pltpu.SemaphoreType.DMA((planes, 3, 2)),
            pltpu.SemaphoreType.DMA((width // columns // divisor(blocks, 8),)),
        ],
        compiler_params=pltpu.CompilerParams(
            collective_id=0, has_side_effects=True, vmem_limit_bytes=67043328
        ),
        name="gathered_hessian",
    )(channel_order, slab_block, attn_partial, residual, norm_gain[None, :], routes, rotation)


def on_device(attn_partial, residual, norm_gain, channel_order, rotation, routes, slab_block):
    experts = lax.axis_size("expert") * lax.axis_size("tensor")
    mean_load = residual.shape[0] * routes.shape[1] // experts
    slots = max(2, mean_load + (mean_load + 1) // 2)
    spread_all = residual.shape[0] <= 4 * slots and lax.axis_size("tensor") == 4
    if spread_all:
        return gathered_hessian(
            attn_partial, residual, norm_gain, channel_order, rotation, routes, slab_block
        )[None]
    summed = lax.psum_scatter(
        attn_partial[0].astype(jnp.float32).astype(jnp.bfloat16),
        "tensor",
        scatter_dimension=0,
        tiled=True,
    ).astype(jnp.float32)
    hidden = residual.astype(jnp.float32) + summed
    scale = lax.rsqrt(jnp.mean(hidden * hidden, axis=1, keepdims=True) + 1e-06)
    normed = (hidden * scale * norm_gain[None, :]).astype(jnp.bfloat16)
    payload = rotate_rows(normed, channel_order, rotation)
    start = slab_block[0] * rotation.shape[1]
    rows, count = dispatch_rows(payload, routes)
    slab = lax.dynamic_slice_in_dim(rows, start, SLAB, 1)
    product = lax.dot_general(
        rows, slab, (((0,), (0,)), ((), ())), preferred_element_type=jnp.float32
    )
    return (product * (2.0 / count)).astype(jnp.bfloat16)[None]


def solution(mesh):
    placed = (
        P("tensor", "expert", None),
        P(("expert", "tensor"), None),
        P(),
        P(),
        P(),
        P(("expert", "tensor"), None),
        P(("expert", "tensor")),
    )
    return jax.shard_map(
        on_device,
        mesh=mesh,
        in_specs=placed,
        out_specs=P(("expert", "tensor"), None, None),
        check_vma=False,
    )
```

```python
import functools

import jax
import jax.numpy as jnp
from jax import lax
from jax.experimental import pallas as pl
from jax.experimental.pallas import tpu as pltpu
from jax.sharding import PartitionSpec as P

SLAB = 512


def rotate_rows(rows, channel_order, rotation):
    moved = jnp.take(rows, channel_order, axis=1)
    blocks = moved.reshape(rows.shape[0], rotation.shape[0], rotation.shape[1])
    out = jnp.einsum("rbi,bij->rbj", blocks, rotation, preferred_element_type=jnp.float32)
    return out.reshape(rows.shape[0], -1).astype(jnp.bfloat16)


def dispatch_rows(payload, routes):
    count_expert = lax.axis_size("expert")
    count_tensor = lax.axis_size("tensor")
    experts = count_expert * count_tensor
    local_rows = payload.shape[0]
    mean_load = local_rows * routes.shape[1] // experts
    slots = max(2, mean_load + (mean_load + 1) // 2)
    expert_ids = jnp.arange(experts, dtype=jnp.int32)
    chosen = jnp.any(routes[:, :, None] == expert_ids[None, None, :], axis=1)
    ranks = jnp.cumsum(chosen.astype(jnp.int32), axis=0) - 1
    slot_ids = jnp.arange(slots, dtype=jnp.int32)
    select = (chosen[:, :, None] & (ranks[:, :, None] == slot_ids[None, None, :])).astype(
        jnp.bfloat16
    )
    occupancy = jnp.sum(select.astype(jnp.float32), axis=0).astype(jnp.bfloat16)
    outgoing = jnp.einsum(
        "rec,rd->ecd", select, payload, preferred_element_type=jnp.float32
    ).astype(jnp.bfloat16)
    outgoing = outgoing.reshape(count_expert, count_tensor, slots, payload.shape[1])
    occupancy = occupancy.reshape(count_expert, count_tensor, slots)
    arrived, filled = (
        lax.all_to_all(
            lax.all_to_all(outgoing, "expert", split_axis=0, concat_axis=0, tiled=True),
            "tensor",
            split_axis=1,
            concat_axis=1,
            tiled=True,
        ),
        lax.all_to_all(
            lax.all_to_all(occupancy, "expert", split_axis=0, concat_axis=0, tiled=True),
            "tensor",
            split_axis=1,
            concat_axis=1,
            tiled=True,
        ),
    )
    rows = arrived.reshape(-1, payload.shape[1])
    count = jnp.sum(filled.astype(jnp.float32))
    return rows, count


def line_order(length):
    orders = []
    for at in range(length):
        near = -1 if 2 * at < length else 1
        hops = [d for far in range(1, length) for d in (near * far, -near * far)]
        orders.append([at + d for d in hops if 0 <= at + d < length])
    return orders


OWN = ("own", 0)
GRAM_PARTS = 2
ORDER = (
    0, 1, 2, 3, 4, 5, 6, 7, 8, 10, 16, 17, 18, 19, 13, 15, 14, 25, 11, 23, 30, 12, 31, 33, 28,
    22, 21, 24, 37, 50, 29, 32, 53, 54, 56, 26, 20, 61, 9, 27, 49, 55, 35, 46, 47, 40, 36, 48,
    52, 45, 51, 76, 42, 85, 34, 57, 70, 75, 38, 77, 69, 74, 73, 44, 59, 79, 39, 43, 58, 60, 71,
    84, 41, 78, 72, 63, 64, 81, 62, 83, 80, 82, 65, 67, 95, 66, 94, 68, 96, 87, 93, 99, 100,
    97, 88, 98, 86, 90, 89, 103, 101, 104, 92, 91, 102, 105, 106,
)


def steps(planes, spans, groups):
    turns = [("turn", k) for k in range(planes - 1)]
    atoms = []

    def relay(z, kind):
        atoms.extend([("rx", z, kind), ("ry", z, kind)])

    def take(far, kind):
        for dx, dy in ((0, 0), (1, 0), (0, 1), (1, 1)) if kind == 2 else ((0, 0),):
            atoms.extend([("take", step, kind, dx, dy) for step in (-far, far)])

    def gram(z, dy):
        atoms.extend([("gram", z, dy, part) for part in range(GRAM_PARTS)])

    def spread(z):
        atoms.extend([("spread", z, kind) for kind in (0, 1)])

    for q in (0, 1):
        atoms.append(("chunk", q))
        kinds = [kind for kind in (2, 0, 1) if spans[kind][0] == q]
        for g in range(len(groups)):
            atoms.append(("rot", q, g))
            for kind in kinds:
                if overlap(spans[kind], groups[g]):
                    atoms.append(("osend", q, g, kind))
        atoms.extend([("oc", kind) for kind in kinds])
    relay(OWN, 0)
    take(1, 0)
    relay(OWN, 2)
    relay(OWN, 1)
    take(1, 1)
    spread(turns[0])
    atoms.extend([("diag", OWN, kind) for kind in (2, 0, 1)])
    take(1, 2)
    for k in range(planes - 1):
        before = turns[k - 1] if k else OWN
        relay(turns[k], 0)
        gram(before, 0)
        if k + 2 < planes:
            take(k + 2, 0)
        relay(turns[k], 1)
        if k + 2 < planes:
            take(k + 2, 1)
            spread(turns[k + 1])
        gram(before, 1)
        atoms.extend([("diag", turns[k], kind) for kind in (0, 1)])
        if k + 2 < planes:
            take(k + 2, 2)
    gram(turns[-1], 0)
    gram(turns[-1], 1)
    return [atoms[i] for i in ORDER] if len(atoms) == len(ORDER) else atoms


def overlap(span, group):
    first, last = max(span[1], group[0]), min(span[2], group[1])
    return (first, last) if first < last else None


def spans_of(every):
    late = every * 26 // 57
    return (
        (0, 0, every), (1, late, every), (1, 0, late),
    )


def groups_of(blocks, every, group):
    edges = list(range(0, blocks, group)) + [every]
    return list(zip(edges[:-1], edges[1:]))


def plan(planes, spans, groups):
    ops = []

    def wait(z, dx, dy, kind, part=None, other=0):
        ops.append(("wait", z, dx, dy, other, kind, part))

    def send(z, dx, dy, kind, part, *ways):
        for way in ways:
            ops.append(("send", z, dx, dy, kind, part, way))

    def up(kind):
        return ("z+", "z-") if kind == 2 else ()

    for atom in steps(planes, spans, groups):
        name = atom[0]
        if name in ("chunk", "rot"):
            ops.append(atom)
        elif name == "osend":
            ways = ("y", "x", "z+", "z-") if atom[3] == 2 else ("z+", "z-", "y", "x")
            send(OWN, 0, 0, atom[3], overlap(spans[atom[3]], groups[atom[2]]), *ways)
        elif name == "oc":
            send(OWN, 0, 0, atom[1], None, "c")
        elif name == "rx":
            wait(atom[1], 1, 0, atom[2])
            send(atom[1], 1, 0, atom[2], 0, "y")
            send(atom[1], 1, 0, atom[2], None, *up(atom[2]), "c")
        elif name == "ry":
            wait(atom[1], 0, 1, atom[2])
            send(atom[1], 0, 1, atom[2], 1, "x")
            send(atom[1], 0, 1, atom[2], None, *up(atom[2]), "c")
        elif name == "diag":
            wait(atom[1], 1, 1, atom[2], 0)
            wait(atom[1], 1, 1, atom[2], 1)
            send(atom[1], 1, 1, atom[2], None, *up(atom[2]), "c")
        elif name == "take":
            step, kind, dx, dy = atom[1:]
            wait(("dist", step), dx, dy, kind)
            send(("dist", step), dx, dy, kind, None, "z+" if step < 0 else "z-", "c")
        elif name == "spread":
            send(atom[1], 0, 0, atom[2], None, "y", "x")
        else:
            if atom[3] == 0:
                for kind in (0, 1, 2):
                    for dx in (0, 1):
                        wait(atom[1], dx, atom[2], kind, None, 1)
            ops.append(atom)
    return ops


def divisor(number, most):
    return max(d for d in range(1, most + 1) if number % d == 0)


def hessian_kernel(
    planes, local, width, columns, extra,
    order_ref, block_ref, partial_ref, residual_ref, gain_ref, routes_ref, rotation_ref, out_ref,
    rows, total, staged, picked, slab, split, rotation, mid, far, residual, moved,
    load_sem, core_send, core_recv, pair_send, pair_recv, send_sem, recv_sem, half_sem, out_sem,
):
    expert, tensor = lax.axis_index("expert"), lax.axis_index("tensor")
    plane, side = lax.div(expert, 2), lax.rem(expert, 2)
    pair, core = lax.div(tensor, 2), lax.rem(tensor, 2)
    me = expert * 4 + tensor
    half = local // 2
    orders = line_order(planes)

    def table(values):
        total_of = 0
        for at, value in enumerate(values):
            total_of = total_of + value * lax.div(
                planes - lax.rem(plane + planes - at, planes), planes
            )
        return total_of

    def device(z, y, x, c):
        return (z * 2 + y, x * 2 + c)

    def remote(source, target, send, recv, to):
        return pltpu.make_async_remote_copy(
            src_ref=source, dst_ref=target, send_sem=send, recv_sem=recv,
            device_id=to, device_id_type=pl.DeviceIdType.MESH,
        )

    other_pair = device(plane, side, 1 - pair, core)
    other_side = device(plane, 1 - side, pair, core)
    other_core = device(plane, side, pair, 1 - core)

    def beside(step):
        there = table([1 if 0 <= at + step < planes else 0 for at in range(planes)])
        return there, table([min(max(at + step, 0), planes - 1) for at in range(planes)])

    parts = 4
    size = local // parts
    mine, got = 0, 2 * local

    def source(p, c, at, count):
        start = pl.multiple_of((p * 2 + c) * local + at, size)
        return partial_ref.at[0, pl.ds(start, count), :]

    loads = [
        pltpu.make_async_copy(
            source(p, core, 0, local),
            picked.at[mine + turn * local:mine + (turn + 1) * local, :],
            load_sem.at[turn],
        )
        for turn, p in enumerate((1 - pair, pair))
    ]
    loads.append(pltpu.make_async_copy(residual_ref, residual, load_sem.at[2]))
    loads.append(pltpu.make_async_copy(rotation_ref, rotation, load_sem.at[3]))
    for copy in loads:
        copy.start()

    barrier = pltpu.get_barrier_semaphore()
    barrier_wait = 3
    for peer in (other_core, other_pair, other_side):
        pl.semaphore_signal(
            barrier, inc=1, device_id=peer, device_id_type=pl.DeviceIdType.MESH
        )
    for step in (-1, 1):
        there, z = beside(step)
        barrier_wait = barrier_wait + there

        @pl.when(there == 1)
        def _():
            pl.semaphore_signal(
                barrier, inc=1, device_id=device(z, side, pair, core),
                device_id_type=pl.DeviceIdType.MESH,
            )

    pl.semaphore_wait(barrier, barrier_wait)

    inside = []
    for turn, p in enumerate((1 - pair, pair)):
        for part in range(parts):
            number = turn * parts + part
            first = got + turn * local + part * size
            inside.append(
                remote(
                    source(p, 1 - core, part * size, size),
                    picked.at[first:first + size, :],
                    core_send.at[number], core_recv.at[number], other_core,
                )
            )
            inside[-1].start()

    named = routes_ref[...]
    index = lax.broadcasted_iota(jnp.int32, (extra, local), 0)
    chosen = named[0:1, :] == index
    for k in range(1, named.shape[0]):
        chosen = chosen | (named[k:k + 1, :] == index)
    own_rows = pl.ds(pl.multiple_of(me * local, local), local)
    rows[own_rows, width:] = jnp.where(chosen, 1.0, 0.0).T.astype(jnp.bfloat16)

    across = []
    loads[0].wait()
    for part in range(parts):
        at = slice(part * size, (part + 1) * size)
        inside[part].wait_recv()
        mid[at, :] = (
            picked[mine + part * size:mine + (part + 1) * size, :].astype(jnp.float32)
            + picked[got + part * size:got + (part + 1) * size, :].astype(jnp.float32)
        ).astype(jnp.bfloat16)
        across.append(
            remote(
                mid.at[at, :], far.at[at, :], pair_send.at[part], pair_recv.at[part], other_pair
            )
        )
        if part > 0:
            across[part - 1].start()
    for copy in loads[1:]:
        copy.wait()
    for part in range(parts):
        inside[parts + part].wait_recv()
    across[parts - 1].start()

    blocks = width // columns
    group = divisor(blocks, 14)

    def chunk(q):
        for part in range(q * parts // 2, (q + 1) * parts // 2):
            at = slice(part * size, (part + 1) * size)
            across[part].wait_recv()
            first = local + part * size
            attn = (
                picked[mine + first:mine + first + size, :].astype(jnp.float32)
                + picked[got + first:got + first + size, :].astype(jnp.float32)
                + far[at, :].astype(jnp.float32)
            )
            hidden = residual[at, :].astype(jnp.float32) + attn
            scale = lax.rsqrt(jnp.mean(hidden * hidden, axis=1, keepdims=True) + 1e-06)
            far[at, :] = (hidden * scale * gain_ref[...]).astype(jnp.bfloat16)

        @pl.loop(0, blocks // group)
        def _(b):
            for j in range(group):
                at = pl.ds(pl.multiple_of((b * group + j) * columns, columns), columns)
                total[0, at, 0:half] = far[q * half:(q + 1) * half, at].astype(jnp.float32).T

    def rotate(q, g):
        place = pl.ds(pl.multiple_of(me * local + q * half, half), half)

        @pl.loop(0, group)
        def _(s):
            base = pl.multiple_of(s * columns, columns)
            origin = (g * group + s) * columns
            for j in range(columns):
                moved[base + j, :] = total[0, order_ref[origin + j], :]

        for j in range(group):
            b = g * group + j
            rows[place, b * columns:(b + 1) * columns] = lax.dot_general(
                moved[j * columns:(j + 1) * columns, 0:half].T.astype(jnp.bfloat16),
                rotation[b], (((1,), (0,)), ((), ())),
                preferred_element_type=jnp.float32,
            ).astype(jnp.bfloat16)

    every = (width + extra) // columns
    spans = spans_of(every)
    groups = groups_of(blocks, every, group)

    def plane_of(z):
        if z[0] == "own":
            return None, plane
        if z[0] == "turn":
            return None, table([orders[at][z[1]] for at in range(planes)])
        return beside(z[1])

    def number_of(z, dx, dy, c):
        y = 1 - side if dy else side
        x = 1 - pair if dx else pair
        return (z * 2 + y) * 4 + x * 2 + c

    def piece(number, kind, part):
        h, first, last = spans[kind]
        middle = first + (last - first) * 54 // 100
        if part == 0:
            last = middle
        elif part == 1:
            first = middle
        elif part is not None:
            first, last = part
        return rows.at[
            pl.ds(pl.multiple_of(number * local + h * half, half), half),
            first * columns:last * columns,
        ]

    def arrival(z, number, kind, part):
        return half_sem.at[z, kind, part] if part in (0, 1) else recv_sem.at[number, kind]

    def under(flag, act):
        if flag is None:
            act()
        else:
            pl.when(flag == 1)(act)

    sends = []

    def send(zref, dx, dy, kind, part, way):
        flag, z = plane_of(zref)
        number = number_of(z, dx, dy, core)
        if way in ("z+", "z-"):
            onward, target = beside(1 if way == "z+" else -1)
            flag = onward if flag is None else flag * onward
            to = device(target, side, pair, core)
        else:
            to = {"x": other_pair, "y": other_side, "c": other_core}[way]
        ref = piece(number, kind, part)
        copy = remote(ref, ref, send_sem.at[len(sends)], arrival(z, number, kind, part), to)
        sends.append((flag, copy))
        under(flag, copy.start)

    def arrive(zref, dx, dy, other, kind, part):
        flag, z = plane_of(zref)
        number = number_of(z, dx, dy, 1 - core if other else core)
        ref = piece(number, kind, part)
        copy = remote(ref, ref, send_sem.at[0], arrival(z, number, kind, part), other_core)
        under(flag, copy.wait_recv)

    tile = columns * divisor(blocks, 14)
    last_tile = columns * divisor(blocks, 8)
    begin = block_ref[0]

    def gram(zref, dy, part, first, last, counted):
        z = plane_of(zref)[1]
        y = 1 - side if dy else side
        base = pl.ds(pl.multiple_of((z * 2 + y) * 4 * local, 4 * local), 4 * local)
        if part == 0:
            for b in range(blocks):
                split[b, :, :] = rows[base, b * columns:(b + 1) * columns]
            named = rows[base, width:].astype(jnp.float32)
            lane = lax.broadcasted_iota(jnp.int32, named.shape, 1)
            chosen = jnp.sum(jnp.where(lane == me, named, 0.0), axis=1, keepdims=True)
            for b in range(SLAB // columns):
                slab[:, b * columns:(b + 1) * columns] = (
                    split[begin + b, :, :].astype(jnp.float32) * chosen
                ).astype(jnp.bfloat16)
            counted = counted + jnp.sum(chosen, axis=0, keepdims=True)
        factor = 2.0 / counted
        wide = last_tile if last else tile
        count = width // wide

        @pl.loop(count * part // GRAM_PARTS, count * (part + 1) // GRAM_PARTS)
        def _(step):
            at = pl.ds(pl.multiple_of(step * wide, wide), wide)
            product = lax.dot_general(
                rows[base, at], slab[...], (((0,), (0,)), ((), ())),
                preferred_element_type=jnp.float32,
            )
            for b in range(SLAB // columns):
                lanes = slice(b * columns, (b + 1) * columns)
                if first:
                    total[b, at, :] = product[:, lanes]
                elif not last:
                    total[b, at, :] += product[:, lanes]
                else:
                    staged[at, lanes] = (
                        (total[b, at, :] + product[:, lanes]) * factor
                    ).astype(jnp.bfloat16)
            if last:
                pltpu.make_async_copy(staged.at[at, :], out_ref.at[at, :], out_sem.at[step]).start()

        return counted

    counted = jnp.zeros((1, 1), jnp.float32)
    grams = 0
    for op in plan(planes, spans, groups):
        if op[0] == "chunk":
            chunk(op[1])
        elif op[0] == "rot":
            rotate(op[1], op[2])
        elif op[0] == "send":
            send(*op[1:])
        elif op[0] == "wait":
            arrive(*op[1:])
        else:
            grams += op[3] == 0
            counted = gram(op[1], op[2], op[3], grams == 1, grams == 2 * planes, counted)

    for copy in inside + across:
        copy.wait_send()
    for flag, copy in sends:
        under(flag, copy.wait_send)

    @pl.loop(0, width // last_tile)
    def _(step):
        at = pl.ds(pl.multiple_of(step * last_tile, last_tile), last_tile)
        pltpu.make_async_copy(staged.at[at, :], out_ref.at[at, :], out_sem.at[step]).wait()


def gathered_hessian(
    attn_partial, residual, norm_gain, channel_order, rotation, routes, slab_block
):
    count_expert, count_tensor = lax.axis_size("expert"), lax.axis_size("tensor")
    experts, planes = count_expert * count_tensor, count_expert // 2
    local, width = residual.shape
    blocks, columns = rotation.shape[0], rotation.shape[1]
    extra = -(-experts // columns) * columns
    half = local // 2
    every = (width + extra) // columns
    groups = groups_of(blocks, every, divisor(blocks, 14))
    sends = sum(op[0] == "send" for op in plan(planes, spans_of(every), groups))
    vmem = pl.BlockSpec(memory_space=pltpu.VMEM)
    smem = pl.BlockSpec(memory_space=pltpu.SMEM)
    whole = pl.BlockSpec(memory_space=pl.ANY)
    return pl.pallas_call(
        functools.partial(hessian_kernel, planes, local, width, columns, extra),
        out_shape=jax.ShapeDtypeStruct((width, SLAB), jnp.bfloat16),
        in_specs=[smem, smem, whole, whole, vmem, vmem, whole],
        out_specs=whole,
        scratch_shapes=[
            pltpu.VMEM((experts * local, width + extra), jnp.bfloat16),
            pltpu.VMEM((SLAB // columns, width, columns), jnp.float32),
            pltpu.VMEM((width, SLAB), jnp.bfloat16),
            pltpu.VMEM((4 * local, width), jnp.bfloat16),
            pltpu.VMEM((4 * local, SLAB), jnp.bfloat16),
            pltpu.VMEM((blocks, 4 * local, columns), jnp.bfloat16),
            pltpu.VMEM(rotation.shape, jnp.bfloat16),
            pltpu.VMEM((local, width), jnp.bfloat16),
            pltpu.VMEM((local, width), jnp.bfloat16),
            pltpu.VMEM((local, width), jnp.bfloat16),
            pltpu.VMEM((columns * divisor(blocks, 14), columns), jnp.float32),
            pltpu.SemaphoreType.DMA((4,)),
            pltpu.SemaphoreType.DMA((8,)),
            pltpu.SemaphoreType.DMA((8,)),
            pltpu.SemaphoreType.DMA((4,)),
            pltpu.SemaphoreType.DMA((4,)),
            pltpu.SemaphoreType.DMA((sends,)),
            pltpu.SemaphoreType.DMA((experts, 3)),
            pltpu.SemaphoreType.DMA((planes, 3, 2)),
            pltpu.SemaphoreType.DMA((width // columns // divisor(blocks, 8),)),
        ],
        compiler_params=pltpu.CompilerParams(
            collective_id=0, has_side_effects=True, vmem_limit_bytes=67043328
        ),
        name="gathered_hessian",
    )(channel_order, slab_block, attn_partial, residual, norm_gain[None, :], routes.T, rotation)


def on_device(attn_partial, residual, norm_gain, channel_order, rotation, routes, slab_block):
    experts = lax.axis_size("expert") * lax.axis_size("tensor")
    mean_load = residual.shape[0] * routes.shape[1] // experts
    slots = max(2, mean_load + (mean_load + 1) // 2)
    spread_all = residual.shape[0] <= 4 * slots and lax.axis_size("tensor") == 4
    if spread_all:
        return gathered_hessian(
            attn_partial, residual, norm_gain, channel_order, rotation, routes, slab_block
        )[None]
    summed = lax.psum_scatter(
        attn_partial[0].astype(jnp.float32).astype(jnp.bfloat16),
        "tensor",
        scatter_dimension=0,
        tiled=True,
    ).astype(jnp.float32)
    hidden = residual.astype(jnp.float32) + summed
    scale = lax.rsqrt(jnp.mean(hidden * hidden, axis=1, keepdims=True) + 1e-06)
    normed = (hidden * scale * norm_gain[None, :]).astype(jnp.bfloat16)
    payload = rotate_rows(normed, channel_order, rotation)
    start = slab_block[0] * rotation.shape[1]
    rows, count = dispatch_rows(payload, routes)
    slab = lax.dynamic_slice_in_dim(rows, start, SLAB, 1)
    product = lax.dot_general(
        rows, slab, (((0,), (0,)), ((), ())), preferred_element_type=jnp.float32
    )
    return (product * (2.0 / count)).astype(jnp.bfloat16)[None]


def solution(mesh):
    placed = (
        P("tensor", "expert", None),
        P(("expert", "tensor"), None),
        P(),
        P(),
        P(),
        P(("expert", "tensor"), None),
        P(("expert", "tensor")),
    )
    return jax.shard_map(
        on_device,
        mesh=mesh,
        in_specs=placed,
        out_specs=P(("expert", "tensor"), None, None),
        check_vma=False,
    )
```

```python
import functools

import jax
import jax.numpy as jnp
from jax import lax
from jax.experimental import pallas as pl
from jax.experimental.pallas import tpu as pltpu
from jax.sharding import PartitionSpec as P

SLAB = 512


def rotate_rows(rows, channel_order, rotation):
    moved = jnp.take(rows, channel_order, axis=1)
    blocks = moved.reshape(rows.shape[0], rotation.shape[0], rotation.shape[1])
    out = jnp.einsum("rbi,bij->rbj", blocks, rotation, preferred_element_type=jnp.float32)
    return out.reshape(rows.shape[0], -1).astype(jnp.bfloat16)


def dispatch_rows(payload, routes):
    count_expert = lax.axis_size("expert")
    count_tensor = lax.axis_size("tensor")
    experts = count_expert * count_tensor
    local_rows = payload.shape[0]
    mean_load = local_rows * routes.shape[1] // experts
    slots = max(2, mean_load + (mean_load + 1) // 2)
    expert_ids = jnp.arange(experts, dtype=jnp.int32)
    chosen = jnp.any(routes[:, :, None] == expert_ids[None, None, :], axis=1)
    ranks = jnp.cumsum(chosen.astype(jnp.int32), axis=0) - 1
    slot_ids = jnp.arange(slots, dtype=jnp.int32)
    select = (chosen[:, :, None] & (ranks[:, :, None] == slot_ids[None, None, :])).astype(
        jnp.bfloat16
    )
    occupancy = jnp.sum(select.astype(jnp.float32), axis=0).astype(jnp.bfloat16)
    outgoing = jnp.einsum(
        "rec,rd->ecd", select, payload, preferred_element_type=jnp.float32
    ).astype(jnp.bfloat16)
    outgoing = outgoing.reshape(count_expert, count_tensor, slots, payload.shape[1])
    occupancy = occupancy.reshape(count_expert, count_tensor, slots)
    arrived, filled = (
        lax.all_to_all(
            lax.all_to_all(outgoing, "expert", split_axis=0, concat_axis=0, tiled=True),
            "tensor",
            split_axis=1,
            concat_axis=1,
            tiled=True,
        ),
        lax.all_to_all(
            lax.all_to_all(occupancy, "expert", split_axis=0, concat_axis=0, tiled=True),
            "tensor",
            split_axis=1,
            concat_axis=1,
            tiled=True,
        ),
    )
    rows = arrived.reshape(-1, payload.shape[1])
    count = jnp.sum(filled.astype(jnp.float32))
    return rows, count


def line_order(length):
    orders = []
    for at in range(length):
        near = -1 if 2 * at < length else 1
        hops = [d for far in range(1, length) for d in (near * far, -near * far)]
        orders.append([at + d for d in hops if 0 <= at + d < length])
    return orders


OWN = ("own", 0)
GRAM_PARTS = 2
ORDER = (
    0, 1, 2, 3, 4, 5, 6, 7, 8, 10, 16, 17, 18, 19, 13, 15, 14, 25, 11, 23, 30, 12, 31, 33, 28,
    22, 21, 24, 37, 50, 29, 32, 53, 54, 56, 26, 20, 61, 9, 27, 49, 55, 35, 46, 47, 40, 36, 48,
    52, 45, 51, 76, 42, 85, 34, 57, 70, 75, 38, 77, 69, 74, 73, 44, 59, 79, 39, 43, 58, 60, 71,
    84, 41, 78, 72, 63, 64, 81, 62, 83, 80, 82, 65, 67, 95, 66, 94, 68, 96, 87, 93, 99, 100,
    97, 88, 98, 86, 90, 89, 103, 101, 104, 92, 91, 102, 105, 106,
)


def steps(planes, spans, groups):
    turns = [("turn", k) for k in range(planes - 1)]
    atoms = []

    def relay(z, kind):
        atoms.extend([("rx", z, kind), ("ry", z, kind)])

    def take(far, kind):
        for dx, dy in ((0, 0), (1, 0), (0, 1), (1, 1)) if kind == 2 else ((0, 0),):
            atoms.extend([("take", step, kind, dx, dy) for step in (-far, far)])

    def gram(z, dy):
        atoms.extend([("gram", z, dy, part) for part in range(GRAM_PARTS)])

    def spread(z):
        atoms.extend([("spread", z, kind) for kind in (0, 1)])

    for q in (0, 1):
        atoms.append(("chunk", q))
        kinds = [kind for kind in (2, 0, 1) if spans[kind][0] == q]
        for g in range(len(groups)):
            atoms.append(("rot", q, g))
            for kind in kinds:
                if overlap(spans[kind], groups[g]):
                    atoms.append(("osend", q, g, kind))
        atoms.extend([("oc", kind) for kind in kinds])
    relay(OWN, 0)
    take(1, 0)
    relay(OWN, 2)
    relay(OWN, 1)
    take(1, 1)
    spread(turns[0])
    atoms.extend([("diag", OWN, kind) for kind in (2, 0, 1)])
    take(1, 2)
    for k in range(planes - 1):
        before = turns[k - 1] if k else OWN
        relay(turns[k], 0)
        gram(before, 0)
        if k + 2 < planes:
            take(k + 2, 0)
        relay(turns[k], 1)
        if k + 2 < planes:
            take(k + 2, 1)
            spread(turns[k + 1])
        gram(before, 1)
        atoms.extend([("diag", turns[k], kind) for kind in (0, 1)])
        if k + 2 < planes:
            take(k + 2, 2)
    gram(turns[-1], 0)
    gram(turns[-1], 1)
    return [atoms[i] for i in ORDER] if len(atoms) == len(ORDER) else atoms


def overlap(span, group):
    first, last = max(span[1], group[0]), min(span[2], group[1])
    return (first, last) if first < last else None


def spans_of(every):
    late = every * 26 // 57
    return (
        (0, 0, every), (1, late, every), (1, 0, late),
    )


def groups_of(blocks, every, group):
    edges = list(range(0, blocks, group)) + [every]
    return list(zip(edges[:-1], edges[1:]))


def plan(planes, spans, groups):
    ops = []

    def wait(z, dx, dy, kind, part=None, other=0):
        ops.append(("wait", z, dx, dy, other, kind, part))

    def send(z, dx, dy, kind, part, *ways):
        for way in ways:
            ops.append(("send", z, dx, dy, kind, part, way))

    def up(kind):
        return ("z+", "z-") if kind == 2 else ()

    for atom in steps(planes, spans, groups):
        name = atom[0]
        if name in ("chunk", "rot"):
            ops.append(atom)
        elif name == "osend":
            ways = ("y", "x", "z+", "z-") if atom[3] == 2 else ("z+", "z-", "y", "x")
            send(OWN, 0, 0, atom[3], overlap(spans[atom[3]], groups[atom[2]]), *ways)
        elif name == "oc":
            send(OWN, 0, 0, atom[1], None, "c")
        elif name == "rx":
            wait(atom[1], 1, 0, atom[2])
            send(atom[1], 1, 0, atom[2], 0, "y")
            send(atom[1], 1, 0, atom[2], None, *up(atom[2]), "c")
        elif name == "ry":
            wait(atom[1], 0, 1, atom[2])
            send(atom[1], 0, 1, atom[2], 1, "x")
            send(atom[1], 0, 1, atom[2], None, *up(atom[2]), "c")
        elif name == "diag":
            wait(atom[1], 1, 1, atom[2], 0)
            wait(atom[1], 1, 1, atom[2], 1)
            send(atom[1], 1, 1, atom[2], None, *up(atom[2]), "c")
        elif name == "take":
            step, kind, dx, dy = atom[1:]
            wait(("dist", step), dx, dy, kind)
            send(("dist", step), dx, dy, kind, None, "z+" if step < 0 else "z-", "c")
        elif name == "spread":
            send(atom[1], 0, 0, atom[2], None, "y", "x")
        else:
            if atom[3] == 0:
                for kind in (0, 1, 2):
                    for dx in (0, 1):
                        wait(atom[1], dx, atom[2], kind, None, 1)
            ops.append(atom)
    return ops


def divisor(number, most):
    return max(d for d in range(1, most + 1) if number % d == 0)


def hessian_kernel(
    planes, local, width, columns, extra,
    order_ref, block_ref, partial_ref, residual_ref, gain_ref, routes_ref, rotation_ref, out_ref,
    rows, total, picked, slab, split, rotation, far, moved,
    load_sem, core_send, core_recv, pair_send, pair_recv, send_sem, recv_sem, half_sem,
):
    expert, tensor = lax.axis_index("expert"), lax.axis_index("tensor")
    plane, side = lax.div(expert, 2), lax.rem(expert, 2)
    pair, core = lax.div(tensor, 2), lax.rem(tensor, 2)
    me = expert * 4 + tensor
    half = local // 2
    orders = line_order(planes)

    def table(values):
        total_of = 0
        for at, value in enumerate(values):
            total_of = total_of + value * lax.div(
                planes - lax.rem(plane + planes - at, planes), planes
            )
        return total_of

    def device(z, y, x, c):
        return (z * 2 + y, x * 2 + c)

    def remote(source, target, send, recv, to):
        return pltpu.make_async_remote_copy(
            src_ref=source, dst_ref=target, send_sem=send, recv_sem=recv,
            device_id=to, device_id_type=pl.DeviceIdType.MESH,
        )

    other_pair = device(plane, side, 1 - pair, core)
    other_side = device(plane, 1 - side, pair, core)
    other_core = device(plane, side, pair, 1 - core)

    def beside(step):
        there = table([1 if 0 <= at + step < planes else 0 for at in range(planes)])
        return there, table([min(max(at + step, 0), planes - 1) for at in range(planes)])

    parts = 4
    size = local // parts
    mine, got = 0, 2 * local

    def source(p, c, at, count):
        start = pl.multiple_of((p * 2 + c) * local + at, size)
        return partial_ref.at[0, pl.ds(start, count), :]

    loads = [
        pltpu.make_async_copy(
            source(p, core, 0, local),
            picked.at[mine + turn * local:mine + (turn + 1) * local, :],
            load_sem.at[turn],
        )
        for turn, p in enumerate((1 - pair, pair))
    ]
    loads.append(pltpu.make_async_copy(rotation_ref, rotation, load_sem.at[3]))
    for copy in loads:
        copy.start()

    barrier = pltpu.get_barrier_semaphore()
    barrier_wait = 3
    for peer in (other_core, other_pair, other_side):
        pl.semaphore_signal(
            barrier, inc=1, device_id=peer, device_id_type=pl.DeviceIdType.MESH
        )
    for step in (-1, 1):
        there, z = beside(step)
        barrier_wait = barrier_wait + there

        @pl.when(there == 1)
        def _():
            pl.semaphore_signal(
                barrier, inc=1, device_id=device(z, side, pair, core),
                device_id_type=pl.DeviceIdType.MESH,
            )

    pl.semaphore_wait(barrier, barrier_wait)

    inside = []
    for turn, p in enumerate((1 - pair, pair)):
        for part in range(parts):
            number = turn * parts + part
            first = got + turn * local + part * size
            inside.append(
                remote(
                    source(p, 1 - core, part * size, size),
                    picked.at[first:first + size, :],
                    core_send.at[number], core_recv.at[number], other_core,
                )
            )
            inside[-1].start()

    named = routes_ref[...]
    index = lax.broadcasted_iota(jnp.int32, (extra, local), 0)
    chosen = named[0:1, :] == index
    for k in range(1, named.shape[0]):
        chosen = chosen | (named[k:k + 1, :] == index)
    own_rows = pl.ds(pl.multiple_of(me * local, local), local)
    rows[own_rows, width:] = jnp.where(chosen, 1.0, 0.0).T.astype(jnp.bfloat16)

    across = []
    loads[0].wait()
    for part in range(parts):
        at = slice(part * size, (part + 1) * size)
        inside[part].wait_recv()
        mid = picked.at[mine + part * size:mine + (part + 1) * size, :]
        mid[...] = (
            picked[mine + part * size:mine + (part + 1) * size, :].astype(jnp.float32)
            + picked[got + part * size:got + (part + 1) * size, :].astype(jnp.float32)
        ).astype(jnp.bfloat16)
        across.append(
            remote(
                mid, far.at[at, :], pair_send.at[part], pair_recv.at[part], other_pair
            )
        )
        if part > 0:
            across[part - 1].start()
    kept = pltpu.make_async_copy(
        residual_ref, picked.at[got:got + local, :], load_sem.at[2]
    )
    kept.start()
    for copy in loads[1:] + [kept]:
        copy.wait()
    for part in range(parts):
        inside[parts + part].wait_recv()
    across[parts - 1].start()

    blocks = width // columns
    group, batch = divisor(blocks, 14), divisor(blocks, 7)

    def chunk(q):
        for part in range(q * parts // 2, (q + 1) * parts // 2):
            at = slice(part * size, (part + 1) * size)
            across[part].wait_recv()
            first = local + part * size
            attn = (
                picked[mine + first:mine + first + size, :].astype(jnp.float32)
                + picked[got + first:got + first + size, :].astype(jnp.float32)
                + far[at, :].astype(jnp.float32)
            )
            hidden = picked[got + part * size:got + (part + 1) * size, :].astype(jnp.float32) + attn
            scale = lax.rsqrt(jnp.mean(hidden * hidden, axis=1, keepdims=True) + 1e-06)
            far[at, :] = (hidden * scale * gain_ref[...]).astype(jnp.bfloat16)

        @pl.loop(0, blocks // group)
        def _(b):
            for j in range(group):
                at = pl.ds(pl.multiple_of((b * group + j) * columns, columns), columns)
                total[0, at, 0:half] = far[q * half:(q + 1) * half, at].astype(jnp.float32).T

    def rotate(q, g):
        place = pl.ds(pl.multiple_of(me * local + q * half, half), half)

        for begin in range(g * group, (g + 1) * group, batch):

            @pl.loop(0, batch)
            def _(s):
                base = pl.multiple_of(s * columns, columns)
                origin = (begin + s) * columns
                for j in range(columns):
                    moved[base + j, :] = total[0, order_ref[origin + j], :]

            for j in range(batch):
                b = begin + j
                rows[place, b * columns:(b + 1) * columns] = lax.dot_general(
                    moved[j * columns:(j + 1) * columns, 0:half].T.astype(jnp.bfloat16),
                    rotation[b], (((1,), (0,)), ((), ())),
                    preferred_element_type=jnp.float32,
                ).astype(jnp.bfloat16)

    every = (width + extra) // columns
    spans = spans_of(every)
    groups = groups_of(blocks, every, group)

    def plane_of(z):
        if z[0] == "own":
            return None, plane
        if z[0] == "turn":
            return None, table([orders[at][z[1]] for at in range(planes)])
        return beside(z[1])

    def number_of(z, dx, dy, c):
        y = 1 - side if dy else side
        x = 1 - pair if dx else pair
        return (z * 2 + y) * 4 + x * 2 + c

    def piece(number, kind, part):
        h, first, last = spans[kind]
        middle = first + (last - first) * 54 // 100
        if part == 0:
            last = middle
        elif part == 1:
            first = middle
        elif part is not None:
            first, last = part
        return rows.at[
            pl.ds(pl.multiple_of(number * local + h * half, half), half),
            first * columns:last * columns,
        ]

    def arrival(z, number, kind, part):
        return half_sem.at[z, kind, part] if part in (0, 1) else recv_sem.at[number, kind]

    def under(flag, act):
        if flag is None:
            act()
        else:
            pl.when(flag == 1)(act)

    sends = []

    def send(zref, dx, dy, kind, part, way):
        flag, z = plane_of(zref)
        number = number_of(z, dx, dy, core)
        if way in ("z+", "z-"):
            onward, target = beside(1 if way == "z+" else -1)
            flag = onward if flag is None else flag * onward
            to = device(target, side, pair, core)
        else:
            to = {"x": other_pair, "y": other_side, "c": other_core}[way]
        ref = piece(number, kind, part)
        copy = remote(ref, ref, send_sem.at[len(sends)], arrival(z, number, kind, part), to)
        sends.append((flag, copy))
        under(flag, copy.start)

    def arrive(zref, dx, dy, other, kind, part):
        flag, z = plane_of(zref)
        number = number_of(z, dx, dy, 1 - core if other else core)
        ref = piece(number, kind, part)
        copy = remote(ref, ref, send_sem.at[0], arrival(z, number, kind, part), other_core)
        under(flag, copy.wait_recv)

    tile = columns * divisor(blocks, 14)
    last_tile = columns * divisor(blocks, 8)
    begin = block_ref[0]

    def gram(zref, dy, part, first, last, counted):
        z = plane_of(zref)[1]
        y = 1 - side if dy else side
        base = pl.ds(pl.multiple_of((z * 2 + y) * 4 * local, 4 * local), 4 * local)
        if part == 0:
            for b in range(blocks):
                split[b, :, :] = rows[base, b * columns:(b + 1) * columns]
            named = rows[base, width:].astype(jnp.float32)
            lane = lax.broadcasted_iota(jnp.int32, named.shape, 1)
            chosen = jnp.sum(jnp.where(lane == me, named, 0.0), axis=1, keepdims=True)
            for b in range(SLAB // columns):
                slab[:, b * columns:(b + 1) * columns] = (
                    split[begin + b, :, :].astype(jnp.float32) * chosen
                ).astype(jnp.bfloat16)
            counted = counted + jnp.sum(chosen, axis=0, keepdims=True)
        factor = 2.0 / counted
        wide = last_tile if last else tile
        count = width // wide

        @pl.loop(count * part // GRAM_PARTS, count * (part + 1) // GRAM_PARTS)
        def _(step):
            at = pl.ds(pl.multiple_of(step * wide, wide), wide)
            product = lax.dot_general(
                rows[base, at], slab[...], (((0,), (0,)), ((), ())),
                preferred_element_type=jnp.float32,
            )
            for b in range(SLAB // columns):
                lanes = slice(b * columns, (b + 1) * columns)
                if first:
                    total[b, at, :] = product[:, lanes]
                elif not last:
                    total[b, at, :] += product[:, lanes]
                else:
                    out_ref[at, lanes] = (
                        (total[b, at, :] + product[:, lanes]) * factor
                    ).astype(jnp.bfloat16)

        return counted

    counted = jnp.zeros((1, 1), jnp.float32)
    grams = 0
    for op in plan(planes, spans, groups):
        if op[0] == "chunk":
            chunk(op[1])
        elif op[0] == "rot":
            rotate(op[1], op[2])
        elif op[0] == "send":
            send(*op[1:])
        elif op[0] == "wait":
            arrive(*op[1:])
        else:
            grams += op[3] == 0
            counted = gram(op[1], op[2], op[3], grams == 1, grams == 2 * planes, counted)

    for copy in inside + across:
        copy.wait_send()
    for flag, copy in sends:
        under(flag, copy.wait_send)


def gathered_hessian(
    attn_partial, residual, norm_gain, channel_order, rotation, routes, slab_block
):
    count_expert, count_tensor = lax.axis_size("expert"), lax.axis_size("tensor")
    experts, planes = count_expert * count_tensor, count_expert // 2
    local, width = residual.shape
    blocks, columns = rotation.shape[0], rotation.shape[1]
    extra = -(-experts // columns) * columns
    half = local // 2
    every = (width + extra) // columns
    groups = groups_of(blocks, every, divisor(blocks, 14))
    sends = sum(op[0] == "send" for op in plan(planes, spans_of(every), groups))
    vmem = pl.BlockSpec(memory_space=pltpu.VMEM)
    smem = pl.BlockSpec(memory_space=pltpu.SMEM)
    whole = pl.BlockSpec(memory_space=pltpu.HBM)
    return pl.pallas_call(
        functools.partial(hessian_kernel, planes, local, width, columns, extra),
        out_shape=pltpu.VMEM((width, SLAB), jnp.bfloat16),
        in_specs=[smem, smem, whole, whole, vmem, vmem, whole],
        out_specs=vmem,
        scratch_shapes=[
            pltpu.VMEM((experts * local, width + extra), jnp.bfloat16),
            pltpu.VMEM((SLAB // columns, width, columns), jnp.float32),
            pltpu.VMEM((4 * local, width), jnp.bfloat16),
            pltpu.VMEM((4 * local, SLAB), jnp.bfloat16),
            pltpu.VMEM((blocks, 4 * local, columns), jnp.bfloat16),
            pltpu.VMEM(rotation.shape, jnp.bfloat16),
            pltpu.VMEM((local, width), jnp.bfloat16),
            pltpu.VMEM((columns * divisor(blocks, 7), columns), jnp.float32),
            pltpu.SemaphoreType.DMA((4,)),
            pltpu.SemaphoreType.DMA((8,)),
            pltpu.SemaphoreType.DMA((8,)),
            pltpu.SemaphoreType.DMA((4,)),
            pltpu.SemaphoreType.DMA((4,)),
            pltpu.SemaphoreType.DMA((sends,)),
            pltpu.SemaphoreType.DMA((experts, 3)),
            pltpu.SemaphoreType.DMA((planes, 3, 2)),
        ],
        compiler_params=pltpu.CompilerParams(
            collective_id=0, has_side_effects=True, vmem_limit_bytes=57000000
        ),
        name="gathered_hessian",
    )(channel_order, slab_block, attn_partial, residual, norm_gain[None, :], routes.T, rotation)


def on_device(attn_partial, residual, norm_gain, channel_order, rotation, routes, slab_block):
    experts = lax.axis_size("expert") * lax.axis_size("tensor")
    mean_load = residual.shape[0] * routes.shape[1] // experts
    slots = max(2, mean_load + (mean_load + 1) // 2)
    spread_all = residual.shape[0] <= 4 * slots and lax.axis_size("tensor") == 4
    if spread_all:
        return gathered_hessian(
            attn_partial, residual, norm_gain, channel_order, rotation, routes, slab_block
        )[None]
    summed = lax.psum_scatter(
        attn_partial[0].astype(jnp.float32).astype(jnp.bfloat16),
        "tensor",
        scatter_dimension=0,
        tiled=True,
    ).astype(jnp.float32)
    hidden = residual.astype(jnp.float32) + summed
    scale = lax.rsqrt(jnp.mean(hidden * hidden, axis=1, keepdims=True) + 1e-06)
    normed = (hidden * scale * norm_gain[None, :]).astype(jnp.bfloat16)
    payload = rotate_rows(normed, channel_order, rotation)
    start = slab_block[0] * rotation.shape[1]
    rows, count = dispatch_rows(payload, routes)
    slab = lax.dynamic_slice_in_dim(rows, start, SLAB, 1)
    product = lax.dot_general(
        rows, slab, (((0,), (0,)), ((), ())), preferred_element_type=jnp.float32
    )
    return (product * (2.0 / count)).astype(jnp.bfloat16)[None]


def solution(mesh):
    placed = (
        P("tensor", "expert", None),
        P(("expert", "tensor"), None),
        P(),
        P(),
        P(),
        P(("expert", "tensor"), None),
        P(("expert", "tensor")),
    )
    return jax.shard_map(
        on_device,
        mesh=mesh,
        in_specs=placed,
        out_specs=P(("expert", "tensor"), None, None),
        check_vma=False,
    )
```
